32 devices in a mesh: seq: 8 (over z, x), head: 4 (over y, core).
Axes of the slice: x: 2, y: 2, z: 4, core: 2. Of those that a mesh axis runs over, the one named last changes fastest.
Arguments:
- queries: bfloat16 [1024, 4096], P(('seq', 'head')), may hold values from -0.5 to 0.5
- keys: bfloat16 [1024, 4096], P(('seq', 'head')), may hold values from -0.5 to 0.5
- values: bfloat16 [1024, 4096], P(('seq', 'head')), may hold values from -6 to 6
- grad_out: bfloat16 [1024, 4096], P(('seq', 'head')), may hold values from -6 to 6
- gates: float32 [1024, 32], P('seq', 'head'), may hold values from -1.5 to 0, as said below
Outputs:
- grad_queries: bfloat16 [1024, 4096], P('seq', 'head')
- grad_keys: bfloat16 [1024, 4096], P('seq', 'head')
- grad_values: bfloat16 [1024, 4096], P('seq', 'head')
The draws below stay inside these ranges and needn't reach their ends.
Inputs may be any that keep to these rules, and one draw needn't show every extreme that they name: gates are negative.
All inputs are finite; a program needn't handle non-finite values.
Results may differ from the reference program's by a relative error of at most 0.0058.
Values may be sent and summed in bfloat16 or wider, within the bound.
A program may use at most 128 MiB of HBM per device.

```python
import math
import jax
import jax.numpy as jnp
from jax import lax

HEAD_COUNT = 32
DH = 128
TOK_DEV = 128
TOKEN_COUNT = 1024
N_SEQ = 8


def draw_gates(key, part):
    pick_key, fast_key, slow_key, rough_key, location_random_key, depth_random_key = jax.random.split(key, 6)
    fast_share = 0.5
    fast_heads = jax.random.uniform(pick_key, (HEAD_COUNT,), jnp.float32) < fast_share
    fast_rate = jnp.exp(jax.random.uniform(fast_key, (HEAD_COUNT,), jnp.float32, math.log(1.0 / 50.0), math.log(1.0 / 30.0)))
    slow_rate = jnp.exp(jax.random.uniform(slow_key, (HEAD_COUNT,), jnp.float32, math.log(0.05 / TOKEN_COUNT), math.log(0.6 / TOKEN_COUNT)))
    per_head_rate = jnp.where(fast_heads, fast_rate, slow_rate)
    jaggedness = jax.random.uniform(rough_key, (TOKEN_COUNT, HEAD_COUNT), jnp.float32, 0.5, 1.5)
    spike_locations = jax.random.randint(location_random_key, (2, HEAD_COUNT), 0, TOKEN_COUNT)
    spike_depth = jnp.log(jax.random.uniform(depth_random_key, (2, HEAD_COUNT), jnp.float32, 0.5, 0.8))
    position_indices = jnp.arange(TOKEN_COUNT)[:, None]
    spike_events = jnp.where(position_indices == spike_locations[0][None, :], spike_depth[0][None, :], 0.0)
    spike_events = spike_events + jnp.where(position_indices == spike_locations[1][None, :], spike_depth[1][None, :], 0.0)
    return (-per_head_rate[None, :] * jaggedness + spike_events).astype(jnp.float32)


def block_levels(own_key, extent, pieces, smallest, top_value):
    factor_of = 1.0
    for dim, blocks in pieces:
        heights = jax.random.uniform(jax.random.fold_in(jax.random.fold_in(own_key, 6), dim), (blocks,), jnp.float32, smallest / len(pieces), top_value / len(pieces))
        factor_of = factor_of * jnp.repeat(jnp.exp(heights), extent[dim] // blocks).reshape((-1,) + (1,) * (len(extent) - 1 - dim))
    return factor_of


def bell_draw(own_key, shape, width, limit, cuts=(), dtype=jnp.bfloat16):
    gain = block_levels(own_key, shape, cuts, -0.22, 0.18) if cuts else 1.0
    values = jax.random.normal(own_key, shape, jnp.float32) * width * gain
    return jnp.minimum(jnp.maximum(values, -limit), limit).astype(dtype)


def setup_inputs(seed: int = 0) -> dict:
    seeds = jax.random.split(jax.random.key(seed), 6)
    return {
        "queries": bell_draw(seeds[0], (TOKEN_COUNT, HEAD_COUNT * DH), DH ** -0.5, 0.5, ((0, 32),)),
        "keys": bell_draw(seeds[1], (TOKEN_COUNT, HEAD_COUNT * DH), DH ** -0.5, 0.5, ((0, 32),)),
        "values": bell_draw(seeds[2], (TOKEN_COUNT, HEAD_COUNT * DH), 1.0, 6.0, ((0, 32),)),
        "grad_out": bell_draw(seeds[3], (TOKEN_COUNT, HEAD_COUNT * DH), 1.0, 6.0, ((0, 32),)),
        "gates": draw_gates(jax.random.fold_in(seeds[5], 71), 0),
    }


HIGHEST_PRECISION = lax.Precision.HIGHEST

def decay_parts(gate_rows):
    cumulated = jnp.cumsum(gate_rows, axis=0)
    block_end = cumulated[-1]
    by_head = cumulated.T
    position_indices = jnp.arange(cumulated.shape[0])
    causal = position_indices[:, None] >= position_indices[None, :]
    log_gaps = jnp.where(causal[None], by_head[:, :, None] - by_head[:, None, :], 0.0)
    decay_table = jnp.where(causal[None], jnp.exp(log_gaps), 0.0)
    return (cumulated, block_end, decay_table)

def reference(queries, keys, values, grad_out, gates):
    block_shape = (N_SEQ, TOK_DEV, HEAD_COUNT, DH)
    query_blocks = queries.reshape(block_shape)
    key_blocks = keys.reshape(block_shape)
    value_blocks = values.reshape(block_shape)
    grad_blocks = grad_out.reshape(block_shape)
    gate_blocks = gates.reshape(N_SEQ, TOK_DEV, HEAD_COUNT)

    def forward_block(carry, inputs):
        prefix_state, prefix_norm = carry
        query_rows, key_rows, value_rows, grad_rows, gate_rows = inputs
        cumulated, block_end, decay_table = decay_parts(gate_rows)
        growth = jnp.exp(cumulated)
        fade_out = jnp.exp(block_end[None, :] - cumulated)
        carry_gain = jnp.exp(block_end)
        norm_total = growth * prefix_norm[None, :] + lax.optimization_barrier(jnp.sum(decay_table, axis=2)).T
        inverse_root = lax.rsqrt(norm_total)
        scaled = (grad_rows.astype(jnp.float32) * inverse_root[:, :, None]).astype(jnp.bfloat16)
        mixing = jnp.einsum('the,she->hts', grad_rows.astype(jnp.float32), value_rows.astype(jnp.float32))
        weighted = (mixing * decay_table * inverse_root.T[:, :, None]).astype(jnp.bfloat16)
        prefix_low = prefix_state.astype(jnp.bfloat16)
        grad_q = jnp.einsum('hts,shd->thd', weighted.astype(jnp.float32), key_rows.astype(jnp.float32))
        grad_q = grad_q + growth[:, :, None] * jnp.einsum('the,hde->thd', scaled.astype(jnp.float32), prefix_low.astype(jnp.float32))
        key_fade = key_rows.astype(jnp.float32) * fade_out[:, :, None]
        local_state = jnp.einsum('thd,the->hde', key_fade, value_rows.astype(jnp.float32), precision=HIGHEST_PRECISION)
        next_state = carry_gain[:, None, None] * prefix_state + local_state
        next_norm = carry_gain * prefix_norm + lax.optimization_barrier(jnp.sum(fade_out, axis=0))
        return ((next_state, next_norm), (grad_q.astype(jnp.bfloat16), scaled, inverse_root))
    start_state = jnp.zeros((HEAD_COUNT, DH, DH), jnp.float32)
    start_norm = jnp.zeros((HEAD_COUNT,), jnp.float32)
    unused, (grad_q_blocks, scaled_blocks, root_blocks) = lax.scan(forward_block, (start_state, start_norm), (query_blocks, key_blocks, value_blocks, grad_blocks, gate_blocks))

    def backward_block(later_state, inputs):
        query_rows, key_rows, value_rows, grad_rows, gate_rows, scaled, inverse_root = inputs
        cumulated, block_end, decay_table = decay_parts(gate_rows)
        growth = jnp.exp(cumulated)
        fade_out = jnp.exp(block_end[None, :] - cumulated)
        carry_gain = jnp.exp(block_end)
        query_wide = query_rows.astype(jnp.float32)
        key_wide = key_rows.astype(jnp.float32)
        value_wide = value_rows.astype(jnp.float32)
        scaled_wide = scaled.astype(jnp.float32)
        mixing = jnp.einsum('the,she->hts', grad_rows.astype(jnp.float32), value_wide)
        weighted = (mixing * decay_table * inverse_root.T[:, :, None]).astype(jnp.bfloat16)
        affinity = (jnp.einsum('thd,shd->hts', query_wide, key_wide) * decay_table).astype(jnp.bfloat16)
        later_low = later_state.astype(jnp.bfloat16).astype(jnp.float32)
        grad_k = jnp.einsum('hts,thd->shd', weighted.astype(jnp.float32), query_wide)
        grad_k = grad_k + fade_out[:, :, None] * jnp.einsum('she,hde->shd', value_wide, later_low)
        grad_v = jnp.einsum('hts,the->she', affinity.astype(jnp.float32), scaled_wide)
        grad_v = grad_v + fade_out[:, :, None] * jnp.einsum('shd,hde->she', key_wide, later_low)
        reach = jnp.einsum('thd,the->hde', query_wide * growth[:, :, None], scaled_wide, precision=HIGHEST_PRECISION)
        next_later = carry_gain[:, None, None] * later_state + reach
        return (next_later, (grad_k.astype(jnp.bfloat16), grad_v.astype(jnp.bfloat16)))
    unused_later, (grad_k_blocks, grad_v_blocks) = lax.scan(backward_block, jnp.zeros((HEAD_COUNT, DH, DH), jnp.float32), (query_blocks, key_blocks, value_blocks, grad_blocks, gate_blocks, scaled_blocks, root_blocks), reverse=True)
    flat_shape = (TOKEN_COUNT, HEAD_COUNT * DH)
    return (grad_q_blocks.reshape(flat_shape), grad_k_blocks.reshape(flat_shape), grad_v_blocks.reshape(flat_shape))
```

```python
import functools

import jax
import jax.numpy as jnp
from jax import lax
from jax.experimental import pallas as pl
from jax.experimental.pallas import tpu as pltpu
from jax.sharding import PartitionSpec as P

DH = 128
SLOW = 4
SPREAD = 1
XLAG = 2
LAG = 2
LEAD = 4

MESH = pl.DeviceIdType.MESH
F32 = jnp.float32
BF16 = jnp.bfloat16
EXACT = lax.Precision.HIGHEST


def dot_nn(x, y):
    return lax.dot_general(x, y, (((1,), (0,)), ((), ())), preferred_element_type=F32)


def dot_nt(x, y):
    return lax.dot_general(x, y, (((1,), (1,)), ((), ())), preferred_element_type=F32)


def dot_tn(x, y):
    return lax.dot_general(x, y, (((0,), (0,)), ((), ())), preferred_element_type=F32)


def fold(count, step, start):
    return step(0, start) if count == 1 else lax.fori_loop(0, count, step, start)


def kernel(
    seq_size, head_size,
    q_ref, k_ref, v_ref, g_ref, gates_ref,
    gq_ref, gk_ref, gv_ref,
    gates, staged, rows, ends, gain, peer_gain, plane_gain,
    table, grow, fade, inner, scaled_ref,
    local, reach, sum_p, sum_n, part_q, part_k, part_v,
    x_send, x_recv, y_send, y_recv, n_send, n_recv, d_recv, acc_p, acc_n, out_rows,
    in_sem, gate_sem, a2a_ssem, a2a_rsem, end_ssem, end_rsem,
    x_ssem, x_rsem, y_ssem, y_rsem, n_ssem, n_rsem, d_ssem, d_rsem, out_sem,
):
    S, H = seq_size, head_size
    A = SLOW
    B = S // A
    RD = q_ref.shape[0]
    T = RD * H
    CW = q_ref.shape[1] // H
    NH = CW // DH
    first = NH - SPREAD
    me_s = lax.axis_index("seq")
    me_h = lax.axis_index("head")
    a = me_s // B
    b = me_s % B
    lo = a * B
    hi = lo + B

    barrier = pltpu.get_barrier_semaphore()
    for r in range(1, H):
        pl.semaphore_signal(
            barrier, inc=1, device_id={"head": (me_h + r) % H}, device_id_type=MESH
        )

    @pl.loop(1, S)
    def _(r):
        pl.semaphore_signal(
            barrier, inc=1, device_id={"seq": (me_s + r) % S}, device_id_type=MESH
        )

    gate_copy = pltpu.make_async_copy(gates_ref, gates, gate_sem)
    gate_copy.start()
    for t, ref in enumerate((q_ref, k_ref, v_ref, g_ref)):
        pltpu.make_async_copy(ref, staged.at[t], in_sem).start()

    t_at = lax.broadcasted_iota(jnp.int32, (T, T), 0)
    s_at = lax.broadcasted_iota(jnp.int32, (T, T), 1)
    causal = t_at >= s_at
    tri = jnp.where(causal, 1.0, 0.0).astype(F32)
    gate_copy.wait()
    c_row = lax.dot_general(
        gates[...], tri, (((1,), (1,)), ((), ())), precision=EXACT, preferred_element_type=F32
    )
    e_col = c_row[:, T - 1 : T]
    norm_col = jnp.sum(jnp.exp(e_col - c_row), axis=1, keepdims=True)
    ends[me_s, 0] = jnp.broadcast_to(norm_col, (NH, DH))
    ends[me_s, 1] = jnp.broadcast_to(e_col, (NH, DH))

    pl.semaphore_wait(barrier, (H - 1) + (S - 1))

    def a2a_copy(h, source, target):
        return pltpu.make_async_remote_copy(
            src_ref=staged.at[:, :, pl.ds(pl.multiple_of(target * CW + h * DH, DH), DH)],
            dst_ref=rows.at[h, :, pl.ds(pl.multiple_of(source * RD, RD), RD), :],
            send_sem=a2a_ssem,
            recv_sem=a2a_rsem.at[h],
            device_id={"head": target},
            device_id_type=MESH,
        )

    def own_copy(h):
        return pltpu.make_async_copy(
            staged.at[:, :, pl.ds(pl.multiple_of(me_h * CW + h * DH, DH), DH)],
            rows.at[h, :, pl.ds(pl.multiple_of(me_h * RD, RD), RD), :],
            a2a_rsem.at[h],
        )

    def send_rows(h):
        for r in range(1, H):
            a2a_copy(h, me_h, (me_h + r) % H).start()
        own_copy(h).start()

    def end_copy(r, source, target):
        return pltpu.make_async_remote_copy(
            src_ref=ends.at[source],
            dst_ref=ends.at[source],
            send_sem=end_ssem,
            recv_sem=end_rsem,
            device_id={"seq": target},
            device_id_type=MESH,
        )

    @pl.loop(1, S)
    def _(r):
        end_copy(r, me_s, (me_s + r) % S).start()

    pltpu.make_async_copy(staged, staged, in_sem).wait()
    send_rows(0)

    @pl.loop(1, LEAD)
    def _(h):
        send_rows(h)

    @pl.when(a == 0)
    def _():
        y_recv[...] = jnp.zeros_like(y_recv)

    @pl.when(a == A - 1)
    def _():
        n_recv[...] = jnp.zeros_like(n_recv)

    c_col = c_row.T
    for h in range(NH):
        col = c_col[:, h : h + 1]
        row = c_row[h : h + 1, :]
        decay = jnp.where(causal, jnp.exp(jnp.where(causal, col - row, 0.0)), 0.0)
        table[h] = decay
        grow[h] = jnp.broadcast_to(jnp.exp(col), (T, DH))
        fade[h] = jnp.broadcast_to(jnp.exp(c_col[T - 1 : T, h : h + 1] - col), (T, DH))
        inner[h] = jnp.broadcast_to(jnp.sum(decay, axis=1, keepdims=True), (T, DH))

    others = ends.at[pl.ds(0, S - 1)]
    pltpu.make_async_copy(others, others, end_rsem).wait()

    zero = jnp.zeros((NH, DH), F32)

    def picked(flag, value):
        return jnp.where(flag, 1.0, 0.0) * value

    def one_block(m, carry):
        pre, suf, norm = carry
        end = ends[m, 1]
        pre = pre + picked((m >= lo) & (m < me_s), end)
        suf = suf + picked((m > me_s) & (m < hi), end)
        earlier = jnp.where(m < me_s, 1.0, 0.0)
        norm = earlier * (norm * jnp.exp(end) + ends[m, 0]) + (1.0 - earlier) * norm
        return (pre, suf, norm)

    pre, suf, norm = lax.fori_loop(0, S, one_block, (zero, zero, zero))
    gain[0] = jnp.exp(pre)
    gain[1] = jnp.exp(suf)
    gain[2] = jnp.exp(pre + suf + ends[me_s, 1])
    gain[3] = norm

    def peer(p):
        return lo + (b + p + 1) % B

    def source_peer(p):
        return lo + (b + B - p - 1) % B

    @pl.loop(0, B - 1)
    def _(p):
        other = source_peer(p)

        def one_end(m, carry):
            before, after, between = carry
            end = ends[m, 1]
            before = before + picked(m < other, end)
            after = after + picked(m > other, end)
            inside = (m > jnp.minimum(me_s, other)) & (m < jnp.maximum(me_s, other))
            between = between + picked(inside, end)
            return (before, after, between)

        before, after, between = lax.fori_loop(lo, hi, one_end, (zero, zero, zero))
        peer_gain[p, 0] = jnp.exp(after)
        peer_gain[p, 1] = picked(other < me_s, jnp.exp(between))
        peer_gain[p, 2] = jnp.exp(before)
        peer_gain[p, 3] = picked(other > me_s, jnp.exp(between))

    @pl.loop(0, A)
    def _(other):
        def one_end(m, between):
            return between + ends[m, 1]

        begin = jnp.minimum(other * B + B, hi)
        stop = jnp.maximum(other * B, lo)
        between = lax.fori_loop(begin, stop, one_end, jnp.where(other < a, 1.0, 0.0) * pre + jnp.where(other > a, 1.0, 0.0) * suf)
        plane_gain[other] = jnp.exp(between)

    def chain_copy(send, recv, ssem, rsem, m, target):
        return pltpu.make_async_remote_copy(
            src_ref=send.at[m],
            dst_ref=recv.at[m],
            send_sem=ssem,
            recv_sem=rsem.at[m],
            device_id={"seq": target},
            device_id_type=MESH,
        )

    def y_copy(m):
        return chain_copy(y_send, y_recv, y_ssem, y_rsem, m, (me_s + B) % S)

    def n_copy(m):
        return chain_copy(n_send, n_recv, n_ssem, n_rsem, m, (me_s + S - B) % S)

    def d_copy(send, m, source, target):
        return pltpu.make_async_remote_copy(
            src_ref=send.at[m],
            dst_ref=d_recv.at[source, m - first],
            send_sem=d_ssem,
            recv_sem=d_rsem.at[source, m - first],
            device_id={"seq": target * B + b},
            device_id_type=MESH,
        )

    def x_copy(p, m, target):
        return pltpu.make_async_remote_copy(
            src_ref=x_send.at[m],
            dst_ref=x_recv.at[p, m],
            send_sem=x_ssem,
            recv_sem=x_rsem.at[m],
            device_id={"seq": target},
            device_id_type=MESH,
        )

    def weight(index, h):
        return gain[index, pl.ds(h, 1), :]

    def peer_weight(p, index, h):
        return peer_gain[p, index, pl.ds(h, 1), :]

    def arrive(m):
        pltpu.make_async_copy(rows.at[m], rows.at[m], a2a_rsem.at[m]).wait()

    def states(m):
        growth = grow[m]
        inverse = lax.rsqrt(growth * weight(3, m) + inner[m])
        inner[m] = inverse
        scaled = (rows[m, 3].astype(F32) * inverse).astype(BF16)
        scaled_ref[m] = scaled
        query_growth = (rows[m, 0].astype(F32) * growth).astype(BF16)
        r_state = dot_tn(query_growth, scaled)
        reach[m] = r_state
        x_send[m, 1] = r_state.astype(BF16)
        key_fade = (rows[m, 1].astype(F32) * fade[m]).astype(BF16)
        l_state = dot_tn(key_fade, rows[m, 2])
        local[m] = l_state
        x_send[m, 0] = l_state.astype(BF16)

        @pl.loop(0, B - 1)
        def _(p):
            x_copy(p, m, peer(p)).start()

    def within(m):
        q, k, v, g = rows[m, 0], rows[m, 1], rows[m, 2], rows[m, 3]
        decay = table[m]
        weighted = (dot_nt(g, v) * decay * inner[m]).astype(BF16)
        affinity = (dot_nt(q, k) * decay).astype(BF16)
        part_q[m] = dot_nn(weighted, k)
        part_k[m] = dot_tn(weighted, q)
        part_v[m] = dot_tn(affinity, scaled_ref[m])

    def plane(m):
        got = x_recv.at[:, m]
        pltpu.make_async_copy(got, got, x_rsem.at[m]).wait()

        @pl.when(a < A - 1)
        def _():
            total = fold(
                B - 1,
                lambda p, x: x + peer_weight(p, 0, m) * x_recv[p, m, 0].astype(F32),
                weight(1, m) * local[m],
            )

            @pl.when(m < first)
            def _():
                sum_p[m] = total

            @pl.when(m >= first)
            def _():
                y_send[m] = total.astype(BF16)

                @pl.loop(a + 1, A)
                def _(target):
                    d_copy(y_send, m, a, target).start()

        @pl.when(a > 0)
        def _():
            total = fold(
                B - 1,
                lambda p, x: x + peer_weight(p, 2, m) * x_recv[p, m, 1].astype(F32),
                weight(0, m) * reach[m],
            )

            @pl.when(m < first)
            def _():
                sum_n[m] = total

            @pl.when(m >= first)
            def _():
                n_send[m] = total.astype(BF16)

                @pl.loop(0, a)
                def _(back):
                    d_copy(n_send, m, a, a - 1 - back).start()

    def hop_up(m):
        @pl.when(a > 0)
        def _():
            y_copy(m).wait_recv()

        @pl.when(a < A - 1)
        def _():
            y_send[m] = (sum_p[m] + weight(2, m) * y_recv[m].astype(F32)).astype(BF16)
            y_copy(m).start()

    def hop_down(m):
        @pl.when(a < A - 1)
        def _():
            n_copy(m).wait_recv()

        @pl.when(a > 0)
        def _():
            n_send[m] = (sum_n[m] + weight(2, m) * n_recv[m].astype(F32)).astype(BF16)
            n_copy(m).start()

    def out_copy(t, m):
        at = pl.ds(pl.multiple_of(m * DH, DH), DH)
        return pltpu.make_async_copy(
            out_rows.at[t, m], (gq_ref, gk_ref, gv_ref)[t].at[:, at], out_sem
        )

    def plane_term(send, other, m):
        d_copy(send, m, other, other).wait_recv()
        return plane_gain[other, pl.ds(m, 1), :] * d_recv[other, m - first].astype(F32)

    def finish(m):
        @pl.when(m < first)
        def _():
            acc_p[...] = weight(0, m) * y_recv[m].astype(F32)
            acc_n[...] = weight(1, m) * n_recv[m].astype(F32)

        @pl.when(m >= first)
        def _():
            acc_p[...] = jnp.zeros_like(acc_p)
            acc_n[...] = jnp.zeros_like(acc_n)

            @pl.loop(0, a)
            def _(back):
                acc_p[...] += plane_term(y_send, a - 1 - back, m)

            @pl.loop(a + 1, A)
            def _(other):
                acc_n[...] += plane_term(n_send, other, m)

        prefix = fold(
            B - 1,
            lambda p, x: x + peer_weight(p, 1, m) * x_recv[p, m, 0].astype(F32),
            acc_p[...],
        ).astype(BF16)
        later = fold(
            B - 1,
            lambda p, x: x + peer_weight(p, 3, m) * x_recv[p, m, 1].astype(F32),
            acc_n[...],
        ).astype(BF16)
        gq = part_q[m] + grow[m] * dot_nt(scaled_ref[m], prefix)
        gk = part_k[m] + fade[m] * dot_nt(rows[m, 2], later)
        gv = part_v[m] + fade[m] * dot_nn(rows[m, 1], later)
        out_rows[0, m] = gq.astype(BF16)
        out_rows[1, m] = gk.astype(BF16)
        out_rows[2, m] = gv.astype(BF16)
        for t in range(3):
            out_copy(t, m).start()

    def guarded(do, m, limit):
        @pl.when((m >= 0) & (m < limit))
        def _():
            do(m)

    last = XLAG + LAG * (A - 1)

    @pl.loop(0, NH + last)
    def _(n):
        @pl.when(n < NH)
        def _():
            arrive(n)

            @pl.when(n + LEAD < NH)
            def _():
                send_rows(n + LEAD)

            states(n)

        @pl.when(n < NH)
        def _():
            within(n)

        guarded(plane, n - XLAG, NH)
        guarded(hop_up, n - XLAG - LAG * a, first)
        guarded(hop_down, n - XLAG - LAG * (A - 1 - a), first)
        guarded(finish, n - last, NH)

    others = ends.at[pl.ds(0, S - 1)]
    pltpu.make_async_copy(others, others, end_ssem).wait()
    sent = staged.at[:, :, pl.ds(0, (H - 1) * CW)]
    pltpu.make_async_copy(sent, sent, a2a_ssem).wait()
    pltpu.make_async_copy(x_recv, x_recv, x_ssem).wait()

    @pl.when(a < A - 1)
    def _():
        pltpu.make_async_copy(y_recv, y_recv, y_ssem).wait()

    @pl.when(a > 0)
    def _():
        pltpu.make_async_copy(n_recv, n_recv, n_ssem).wait()

    spread = d_recv.at[pl.ds(0, A - 1)]
    pltpu.make_async_copy(spread, spread, d_ssem).wait()
    pltpu.make_async_copy(out_rows, out_rows, out_sem).wait()


def hand_over(x_ref, y_ref, z_ref, x_out, y_out, z_out, sems):
    sources, targets = (x_ref, y_ref, z_ref), (x_out, y_out, z_out)
    stores = [pltpu.make_async_copy(sources[i], targets[i], sems.at[i]) for i in range(3)]
    for store in stores:
        store.start()
    for store in stores:
        store.wait()


def body(seq_size, head_size, queries, keys, values, grad_out, gates):
    S, H = seq_size, head_size
    B = S // SLOW
    RD, width = queries.shape
    T = RD * H
    CW = width // H
    NH = CW // DH
    first = NH - SPREAD
    square = (NH, T, DH)
    state = (NH, DH, DH)
    one = (DH, DH)
    vmem = pltpu.VMEM
    dma = pltpu.SemaphoreType.DMA
    anywhere = pl.BlockSpec(memory_space=pl.ANY)
    in_hbm = pl.BlockSpec(memory_space=pltpu.HBM)
    out = jax.ShapeDtypeStruct((T, CW), BF16)
    inputs = [
        pltpu.with_memory_space_constraint(x, pltpu.HBM)
        for x in (queries, keys, values, grad_out, gates.T)
    ]
    results = pl.pallas_call(
        functools.partial(kernel, S, H),
        out_shape=(out, out, out),
        in_specs=[in_hbm] * 5,
        out_specs=(anywhere,) * 3,
        scratch_shapes=[
            vmem((NH, T), F32),
            vmem((4, RD, width), BF16),
            vmem((NH, 4, T, DH), BF16),
            vmem((S, 2, NH, DH), F32),
            vmem((4, NH, DH), F32),
            vmem((B - 1, 4, NH, DH), F32),
            vmem((SLOW, NH, DH), F32),
            vmem((NH, T, T), F32),
            vmem(square, F32),
            vmem(square, F32),
            vmem(square, F32),
            vmem(square, BF16),
            vmem(state, F32),
            vmem(state, F32),
            vmem((first,) + one, F32),
            vmem((first,) + one, F32),
            vmem(square, F32),
            vmem(square, F32),
            vmem(square, F32),
            vmem((NH, 2) + one, BF16),
            vmem((B - 1, NH, 2) + one, BF16),
            vmem(state, BF16),
            vmem((first,) + one, BF16),
            vmem(state, BF16),
            vmem((first,) + one, BF16),
            vmem((SLOW, SPREAD) + one, BF16),
            vmem(one, F32),
            vmem(one, F32),
            vmem((3,) + square, BF16),
            dma,
            dma,
            dma,
            dma((NH,)),
            dma,
            dma,
            dma,
            dma((NH,)),
            dma,
            dma((first,)),
            dma,
            dma((first,)),
            dma,
            dma((SLOW, SPREAD)),
            dma,
        ],
        compiler_params=pltpu.CompilerParams(
            collective_id=0,
            has_side_effects=True,
            vmem_limit_bytes=24 << 20,
        ),
    )(*inputs)
    return pl.pallas_call(
        hand_over,
        out_shape=(out, out, out),
        in_specs=[anywhere] * 3,
        out_specs=(in_hbm,) * 3,
        scratch_shapes=[dma((3,))],
        compiler_params=pltpu.CompilerParams(vmem_limit_bytes=4 << 20),
    )(*results)


def solution(mesh):
    placed = (
        P(("seq", "head"), None),
        P(("seq", "head"), None),
        P(("seq", "head"), None),
        P(("seq", "head"), None),
        P("seq", "head"),
    )
    return jax.shard_map(
        functools.partial(body, mesh.shape["seq"], mesh.shape["head"]),
        mesh=mesh,
        in_specs=placed,
        out_specs=(P("seq", "head"), P("seq", "head"), P("seq", "head")),
        check_vma=False,
    )
```

```python
import functools

import jax
import jax.numpy as jnp
from jax import lax
from jax.experimental import pallas as pl
from jax.experimental.pallas import tpu as pltpu
from jax.sharding import PartitionSpec as P

DH = 128
SLOW = 4
SPREAD = 1
XLAG = 3
HOPS = (0, 5, 4, 0)
FINS = (10, 13, 13, 10)
LEAD = 4

MESH = pl.DeviceIdType.MESH
F32 = jnp.float32
BF16 = jnp.bfloat16
EXACT = lax.Precision.HIGHEST


def dot_nn(x, y):
    return lax.dot_general(x, y, (((1,), (0,)), ((), ())), preferred_element_type=F32)


def dot_nt(x, y):
    return lax.dot_general(x, y, (((1,), (1,)), ((), ())), preferred_element_type=F32)


def dot_tn(x, y):
    return lax.dot_general(x, y, (((0,), (0,)), ((), ())), preferred_element_type=F32)


def fold(count, step, start):
    return step(0, start) if count == 1 else lax.fori_loop(0, count, step, start)


def kernel(
    seq_size, head_size,
    q_ref, k_ref, v_ref, g_ref, gates_ref,
    gq_ref, gk_ref, gv_ref,
    gates, staged, rows, ends, gain, peer_gain, plane_gain,
    table, grow, fade, inner, scaled_ref,
    local, reach, sum_p, sum_n, part_q, part_k, part_v,
    x_send, x_recv, y_send, y_recv, n_send, n_recv, dn_send, d_recv, acc_p, acc_n, out_rows,
    in_sem, gate_sem, a2a_ssem, a2a_rsem, end_ssem, end_rsem,
    x_ssem, x_rsem, y_ssem, y_rsem, n_ssem, n_rsem, dn_ssem, d_rsem, out_sem,
):
    S, H = seq_size, head_size
    A = SLOW
    B = S // A
    RD = q_ref.shape[0]
    T = RD * H
    CW = q_ref.shape[1] // H
    NH = CW // DH
    first = NH - SPREAD
    me_s = lax.axis_index("seq")
    me_h = lax.axis_index("head")
    a = me_s // B
    b = me_s % B
    lo = a * B
    hi = lo + B

    barrier = pltpu.get_barrier_semaphore()
    for r in range(1, H):
        pl.semaphore_signal(
            barrier, inc=1, device_id={"head": (me_h + r) % H}, device_id_type=MESH
        )

    @pl.loop(1, S)
    def _(r):
        pl.semaphore_signal(
            barrier, inc=1, device_id={"seq": (me_s + r) % S}, device_id_type=MESH
        )

    gate_copy = pltpu.make_async_copy(gates_ref, gates, gate_sem)
    gate_copy.start()
    for t, ref in enumerate((q_ref, g_ref, k_ref, v_ref)):
        pltpu.make_async_copy(ref, staged.at[t], in_sem).start()

    t_at = lax.broadcasted_iota(jnp.int32, (T, T), 0)
    s_at = lax.broadcasted_iota(jnp.int32, (T, T), 1)
    causal = t_at >= s_at
    tri = jnp.where(causal, 1.0, 0.0).astype(F32)
    gate_copy.wait()
    c_row = lax.dot_general(
        gates[...], tri, (((1,), (1,)), ((), ())), precision=EXACT, preferred_element_type=F32
    )
    e_col = c_row[:, T - 1 : T]
    norm_col = jnp.sum(jnp.exp(e_col - c_row), axis=1, keepdims=True)
    ends[me_s, 0] = jnp.broadcast_to(norm_col, (NH, DH))
    ends[me_s, 1] = jnp.broadcast_to(e_col, (NH, DH))

    pl.semaphore_wait(barrier, (H - 1) + (S - 1))

    def half(i):
        return pl.ds(2 * i, 2)

    def a2a_copy(h, i, source, target):
        return pltpu.make_async_remote_copy(
            src_ref=staged.at[half(i), :, pl.ds(pl.multiple_of(target * CW + h * DH, DH), DH)],
            dst_ref=rows.at[h, half(i), pl.ds(pl.multiple_of(source * RD, RD), RD), :],
            send_sem=a2a_ssem,
            recv_sem=a2a_rsem.at[h, i],
            device_id={"head": target},
            device_id_type=MESH,
        )

    def own_copy(h, i):
        return pltpu.make_async_copy(
            staged.at[half(i), :, pl.ds(pl.multiple_of(me_h * CW + h * DH, DH), DH)],
            rows.at[h, half(i), pl.ds(pl.multiple_of(me_h * RD, RD), RD), :],
            a2a_rsem.at[h, i],
        )

    def send_half(h, i):
        for r in range(1, H):
            a2a_copy(h, i, me_h, (me_h + r) % H).start()
        own_copy(h, i).start()

    def send_rows(h):
        send_half(h, 0)
        send_half(h, 1)

    def end_copy(r, source, target):
        return pltpu.make_async_remote_copy(
            src_ref=ends.at[source],
            dst_ref=ends.at[source],
            send_sem=end_ssem,
            recv_sem=end_rsem,
            device_id={"seq": target},
            device_id_type=MESH,
        )

    @pl.loop(1, S)
    def _(r):
        end_copy(r, me_s, (me_s + r) % S).start()

    pltpu.make_async_copy(staged, staged, in_sem).wait()
    send_half(0, 1)
    send_half(0, 0)

    @pl.loop(1, LEAD)
    def _(h):
        send_rows(h)

    c_col = c_row.T
    for h in range(NH):
        col = c_col[:, h : h + 1]
        row = c_row[h : h + 1, :]
        decay = jnp.where(causal, jnp.exp(jnp.where(causal, col - row, 0.0)), 0.0)
        table[h] = decay
        grow[h] = jnp.broadcast_to(jnp.exp(col), (T, DH))
        fade[h] = jnp.broadcast_to(jnp.exp(c_col[T - 1 : T, h : h + 1] - col), (T, DH))
        inner[h] = jnp.broadcast_to(jnp.sum(decay, axis=1, keepdims=True), (T, DH))

    def picked(flag, value):
        return jnp.where(flag, 1.0, 0.0) * value

    def take_norm():
        others = ends.at[pl.ds(0, S - 1)]
        pltpu.make_async_copy(others, others, end_rsem).wait()
        gain[3] = lax.fori_loop(
            0,
            me_s,
            lambda m, norm: norm * jnp.exp(ends[m, 1]) + ends[m, 0],
            jnp.zeros((NH, DH), F32),
        )

    def summed(begin, stop, start):
        return lax.fori_loop(begin, stop, lambda m, x: x + ends[m, 1], start)

    def peer(p):
        return lo + (b + p + 1) % B

    def source_peer(p):
        return lo + (b + B - p - 1) % B

    def take_gains():
        zero = jnp.zeros((NH, DH), F32)
        pre = summed(lo, me_s, zero)
        suf = summed(me_s + 1, hi, zero)
        whole = pre + suf + ends[me_s, 1]
        gain[0] = jnp.exp(pre)
        gain[1] = jnp.exp(suf)
        gain[2] = jnp.exp(whole)

        @pl.loop(0, B - 1)
        def _(p):
            other = source_peer(p)
            low = jnp.minimum(me_s, other)
            between = summed(low + 1, jnp.maximum(me_s, other), zero)
            peer_gain[p, 0] = jnp.exp(summed(other + 1, hi, zero))
            peer_gain[p, 1] = picked(other < me_s, jnp.exp(between))
            peer_gain[p, 2] = jnp.exp(summed(lo, other, zero))
            peer_gain[p, 3] = picked(other > me_s, jnp.exp(between))

        @pl.loop(0, A - 1)
        def _(d):
            edge = jnp.where(a == 0, hi, lo - d * B)
            start = jnp.where(a == 0, 1.0, 0.0) * suf + jnp.where(a == 0, 0.0, 1.0) * pre
            stop = jnp.where(a == 0, hi + d * B, lo)

            @pl.when((a == 0) | (a == A - 1))
            def _():
                plane_gain[d] = jnp.exp(summed(edge, stop, start))

    def z_copy(src, dst, ssem, rsem, plane_index):
        return pltpu.make_async_remote_copy(
            src_ref=src,
            dst_ref=dst,
            send_sem=ssem,
            recv_sem=rsem,
            device_id={"seq": plane_index * B + b},
            device_id_type=MESH,
        )

    def y_copy(m):
        return z_copy(y_send.at[m], y_recv.at[m], y_ssem, y_rsem.at[m], (a + 1) % A)

    def n_copy(m):
        return z_copy(n_send.at[m], n_recv.at[m], n_ssem, n_rsem.at[m], (a + A - 1) % A)

    def d_copy(src, ssem, m, slot, target):
        return z_copy(src, d_recv.at[slot, m], ssem, d_rsem.at[m], target)

    def x_copy(p, m, i, target):
        return pltpu.make_async_remote_copy(
            src_ref=x_send.at[m, i],
            dst_ref=x_recv.at[p, m, i],
            send_sem=x_ssem,
            recv_sem=x_rsem.at[m, i],
            device_id={"seq": target},
            device_id_type=MESH,
        )

    def x_start(m, i):
        @pl.loop(0, B - 1)
        def _(p):
            x_copy(p, m, i, peer(p)).start()

    def x_wait(m, i):
        got = x_recv.at[:, m, i]
        pltpu.make_async_copy(got, got, x_rsem.at[m, i]).wait()

    def weight(index, h):
        return gain[index, pl.ds(h, 1), :]

    def peer_weight(p, index, h):
        return peer_gain[p, index, pl.ds(h, 1), :]

    def arrive(m, i):
        got = rows.at[m, half(i)]
        pltpu.make_async_copy(got, got, a2a_rsem.at[m, i]).wait()

    def key_state(m):
        arrive(m, 1)
        key_fade = (rows[m, 2].astype(F32) * fade[m]).astype(BF16)
        l_state = dot_tn(key_fade, rows[m, 3])
        local[m] = l_state
        x_send[m, 0] = l_state.astype(BF16)
        x_start(m, 0)

    def query_state(m):
        arrive(m, 0)
        growth = grow[m]
        inverse = lax.rsqrt(growth * weight(3, m) + inner[m])
        inner[m] = inverse
        scaled = (rows[m, 1].astype(F32) * inverse).astype(BF16)
        scaled_ref[m] = scaled
        query_growth = (rows[m, 0].astype(F32) * growth).astype(BF16)
        r_state = dot_tn(query_growth, scaled)
        reach[m] = r_state
        x_send[m, 1] = r_state.astype(BF16)
        x_start(m, 1)

    def within(m):
        q, g, k, v = rows[m, 0], rows[m, 1], rows[m, 2], rows[m, 3]
        decay = table[m]
        weighted = (dot_nt(g, v) * decay * inner[m]).astype(BF16)
        affinity = (dot_nt(q, k) * decay).astype(BF16)
        part_q[m] = dot_nn(weighted, k)
        part_k[m] = dot_tn(weighted, q)
        part_v[m] = dot_tn(affinity, scaled_ref[m])

    def plane(m):
        x_wait(m, 1)

        @pl.when(a > 0)
        def _():
            total = fold(
                B - 1,
                lambda p, x: x + peer_weight(p, 2, m) * x_recv[p, m, 1].astype(F32),
                weight(0, m) * reach[m],
            )

            @pl.when(a == 2)
            def _():
                sum_n[m] = total

                @pl.when(m >= first)
                def _():
                    dn_send[m - first] = total.astype(BF16)
                    d_copy(dn_send.at[m - first], n_ssem, m, 1, 0).start()

            @pl.when(a != 2)
            def _():
                n_send[m] = total.astype(BF16)

            @pl.when(a == 1)
            def _():
                d_copy(n_send.at[m], n_ssem, m, 0, 0).start()

            @pl.when(a == 3)
            def _():
                @pl.when(m >= first)
                def _():
                    d_copy(n_send.at[m], dn_ssem, m, 2, 0).start()

                n_copy(m).start()

        x_wait(m, 0)

        @pl.when(a < A - 1)
        def _():
            total = fold(
                B - 1,
                lambda p, x: x + peer_weight(p, 0, m) * x_recv[p, m, 0].astype(F32),
                weight(1, m) * local[m],
            )

            @pl.when(a == 1)
            def _():
                sum_p[m] = total

            @pl.when(a != 1)
            def _():
                y_send[m] = total.astype(BF16)

            @pl.when(a == 0)
            def _():
                y_copy(m).start()

            @pl.when(a == 2)
            def _():
                d_copy(y_send.at[m], y_ssem, m, 0, A - 1).start()

    def hop_up(m):
        y_copy(m).wait_recv()
        y_send[m] = (sum_p[m] + weight(2, m) * y_recv[m].astype(F32)).astype(BF16)
        d_copy(y_send.at[m], y_ssem, m, 1, A - 1).start()
        y_copy(m).start()

    def hop_down(m):
        n_copy(m).wait_recv()
        n_send[m] = (sum_n[m] + weight(2, m) * n_recv[m].astype(F32)).astype(BF16)

        @pl.when(m < first)
        def _():
            d_copy(n_send.at[m], n_ssem, m, 1, 0).start()

        n_copy(m).start()

    def hop(m):
        @pl.when(a == 1)
        def _():
            hop_up(m)

        @pl.when(a == 2)
        def _():
            hop_down(m)

    def out_copy(t, m):
        at = pl.ds(pl.multiple_of(m * DH, DH), DH)
        return pltpu.make_async_copy(
            out_rows.at[t, m], (gq_ref, gk_ref, gv_ref)[t].at[:, at], out_sem
        )

    def direct(m, count):
        got = d_recv.at[pl.ds(0, count), m]
        pltpu.make_async_copy(got, got, d_rsem.at[m]).wait()
        total = plane_gain[0, pl.ds(m, 1), :] * d_recv[0, m].astype(F32)
        for d in range(1, count):
            total += plane_gain[d, pl.ds(m, 1), :] * d_recv[d, m].astype(F32)
        return total

    def finish(m):
        @pl.when(a == 2)
        def _():
            y_copy(m).wait_recv()

        @pl.when(a == 1)
        def _():
            n_copy(m).wait_recv()

        @pl.when((a == 1) | (a == 2))
        def _():
            acc_p[...] = weight(0, m) * y_recv[m].astype(F32)
            acc_n[...] = weight(1, m) * n_recv[m].astype(F32)

        @pl.when(a == A - 1)
        def _():
            acc_p[...] = direct(m, 2)
            acc_n[...] = jnp.zeros_like(acc_n)

        @pl.when((a == 0) & (m < first))
        def _():
            acc_p[...] = jnp.zeros_like(acc_p)
            acc_n[...] = direct(m, 2)

        @pl.when((a == 0) & (m >= first))
        def _():
            acc_p[...] = jnp.zeros_like(acc_p)
            acc_n[...] = direct(m, 3)

        prefix = fold(
            B - 1,
            lambda p, x: x + peer_weight(p, 1, m) * x_recv[p, m, 0].astype(F32),
            acc_p[...],
        ).astype(BF16)
        later = fold(
            B - 1,
            lambda p, x: x + peer_weight(p, 3, m) * x_recv[p, m, 1].astype(F32),
            acc_n[...],
        ).astype(BF16)
        gq = part_q[m] + grow[m] * dot_nt(scaled_ref[m], prefix)
        gk = part_k[m] + fade[m] * dot_nt(rows[m, 3], later)
        gv = part_v[m] + fade[m] * dot_nn(rows[m, 2], later)
        out_rows[0, m] = gq.astype(BF16)
        out_rows[1, m] = gk.astype(BF16)
        out_rows[2, m] = gv.astype(BF16)
        for t in range(3):
            out_copy(t, m).start()

    def guarded(do, m, limit):
        @pl.when((m >= 0) & (m < limit))
        def _():
            do(m)

    def by_plane(values):
        return sum(jnp.where(a == i, value, 0) for i, value in enumerate(values))

    fin_lag, hop_lag = by_plane(FINS), by_plane(HOPS)

    @pl.loop(0, NH + fin_lag)
    def _(n):
        @pl.when(n == 0)
        def _():
            key_state(0)
            take_norm()

        @pl.when(n < NH)
        def _():
            @pl.when(n + LEAD < NH)
            def _():
                send_rows(n + LEAD)

            query_state(n)

        @pl.when((n > 0) & (n < NH))
        def _():
            key_state(n)

        @pl.when(n == 0)
        def _():
            take_gains()

        guarded(plane, n - XLAG, NH)
        guarded(hop, n - hop_lag, NH)
        @pl.when(n < NH)
        def _():
            within(n)

        guarded(finish, n - fin_lag, NH)

    others = ends.at[pl.ds(0, S - 1)]
    pltpu.make_async_copy(others, others, end_ssem).wait()
    sent = staged.at[:, :, pl.ds(0, (H - 1) * CW)]
    pltpu.make_async_copy(sent, sent, a2a_ssem).wait()
    pltpu.make_async_copy(x_recv, x_recv, x_ssem).wait()

    def sent_all(ref, sem):
        pltpu.make_async_copy(ref, ref, sem).wait()

    @pl.when((a == 0) | (a == 2))
    def _():
        sent_all(d_recv.at[0], y_ssem)

    @pl.when(a == 1)
    def _():
        sent_all(d_recv.at[pl.ds(0, 2)], y_ssem)

    @pl.when((a == 1) | (a == 3))
    def _():
        sent_all(d_recv.at[0], n_ssem)

    @pl.when(a == 2)
    def _():
        sent_all(d_recv.at[pl.ds(0, 2)], n_ssem)

    @pl.when(a == 3)
    def _():
        sent_all(dn_send, dn_ssem)

    pltpu.make_async_copy(out_rows, out_rows, out_sem).wait()


def hand_over(x_ref, y_ref, z_ref, x_out, y_out, z_out, sems):
    sources, targets = (x_ref, y_ref, z_ref), (x_out, y_out, z_out)
    stores = [pltpu.make_async_copy(sources[i], targets[i], sems.at[i]) for i in range(3)]
    for store in stores:
        store.start()
    for store in stores:
        store.wait()


def body(seq_size, head_size, queries, keys, values, grad_out, gates):
    S, H = seq_size, head_size
    B = S // SLOW
    RD, width = queries.shape
    T = RD * H
    CW = width // H
    NH = CW // DH
    square = (NH, T, DH)
    state = (NH, DH, DH)
    one = (DH, DH)
    vmem = pltpu.VMEM
    dma = pltpu.SemaphoreType.DMA
    anywhere = pl.BlockSpec(memory_space=pl.ANY)
    in_hbm = pl.BlockSpec(memory_space=pltpu.HBM)
    out = jax.ShapeDtypeStruct((T, CW), BF16)
    inputs = [
        pltpu.with_memory_space_constraint(x, pltpu.HBM)
        for x in (queries, keys, values, grad_out, gates.T)
    ]
    results = pl.pallas_call(
        functools.partial(kernel, S, H),
        out_shape=(out, out, out),
        in_specs=[in_hbm] * 5,
        out_specs=(anywhere,) * 3,
        scratch_shapes=[
            vmem((NH, T), F32),
            vmem((4, RD, width), BF16),
            vmem((NH, 4, T, DH), BF16),
            vmem((S, 2, NH, DH), F32),
            vmem((4, NH, DH), F32),
            vmem((B - 1, 4, NH, DH), F32),
            vmem((SLOW - 1, NH, DH), F32),
            vmem((NH, T, T), F32),
            vmem(square, F32),
            vmem(square, F32),
            vmem(square, F32),
            vmem(square, BF16),
            vmem(state, F32),
            vmem(state, F32),
            vmem(state, F32),
            vmem(state, F32),
            vmem(square, F32),
            vmem(square, F32),
            vmem(square, F32),
            vmem((NH, 2) + one, BF16),
            vmem((B - 1, NH, 2) + one, BF16),
            vmem(state, BF16),
            vmem(state, BF16),
            vmem(state, BF16),
            vmem(state, BF16),
            vmem((SPREAD,) + one, BF16),
            vmem((SLOW - 1,) + state, BF16),
            vmem(one, F32),
            vmem(one, F32),
            vmem((3,) + square, BF16),
            dma,
            dma,
            dma,
            dma((NH, 2)),
            dma,
            dma,
            dma,
            dma((NH, 2)),
            dma,
            dma((NH,)),
            dma,
            dma((NH,)),
            dma,
            dma((NH,)),
            dma,
        ],
        compiler_params=pltpu.CompilerParams(
            collective_id=0,
            has_side_effects=True,
            vmem_limit_bytes=24 << 20,
        ),
    )(*inputs)
    return pl.pallas_call(
        hand_over,
        out_shape=(out, out, out),
        in_specs=[anywhere] * 3,
        out_specs=(in_hbm,) * 3,
        scratch_shapes=[dma((3,))],
        compiler_params=pltpu.CompilerParams(vmem_limit_bytes=4 << 20),
    )(*results)


def solution(mesh):
    placed = (
        P(("seq", "head"), None),
        P(("seq", "head"), None),
        P(("seq", "head"), None),
        P(("seq", "head"), None),
        P("seq", "head"),
    )
    return jax.shard_map(
        functools.partial(body, mesh.shape["seq"], mesh.shape["head"]),
        mesh=mesh,
        in_specs=placed,
        out_specs=(P("seq", "head"), P("seq", "head"), P("seq", "head")),
        check_vma=False,
    )
```

```python
import functools

import jax
import jax.numpy as jnp
from jax import lax
from jax.experimental import pallas as pl
from jax.experimental.pallas import tpu as pltpu
from jax.sharding import PartitionSpec as P

DH = 128
SLOW = 4
XLAG = 3
HOPS = (0, 4, 4, 0)
FINS = (10, 11, 11, 10)
LEAD = 8

MESH = pl.DeviceIdType.MESH
F32 = jnp.float32
BF16 = jnp.bfloat16
EXACT = lax.Precision.HIGHEST


def dot_nn(x, y):
    return lax.dot_general(x, y, (((1,), (0,)), ((), ())), preferred_element_type=F32)


def dot_nt(x, y):
    return lax.dot_general(x, y, (((1,), (1,)), ((), ())), preferred_element_type=F32)


def dot_tn(x, y):
    return lax.dot_general(x, y, (((0,), (0,)), ((), ())), preferred_element_type=F32)


def fold(count, step, start):
    return step(0, start) if count == 1 else lax.fori_loop(0, count, step, start)


def kernel(
    seq_size, head_size,
    q_ref, k_ref, v_ref, g_ref, gates_ref,
    gq_ref, gk_ref, gv_ref,
    gates, staged, rows, ends, gain, peer_gain, plane_gain,
    table, grow, fade, inner, scaled_ref,
    local, reach, sum_p, sum_n, part_q, part_k, part_v,
    x_send, x_recv, y_send, y_recv, n_send, n_recv, d_recv, acc_p, acc_n,
    in_sem, gate_sem, a2a_ssem, a2a_rsem, end_ssem, end_rsem,
    x_ssem, x_rsem, y_ssem, y_rsem, n_ssem, n_rsem,
):
    S, H = seq_size, head_size
    A = SLOW
    B = S // A
    RD = q_ref.shape[0]
    T = RD * H
    CW = q_ref.shape[1] // H
    NH = CW // DH
    me_s = lax.axis_index("seq")
    me_h = lax.axis_index("head")
    a = me_s // B
    b = me_s % B
    lo = a * B
    hi = lo + B

    barrier = pltpu.get_barrier_semaphore()
    for r in range(1, H):
        pl.semaphore_signal(
            barrier, inc=1, device_id={"head": (me_h + r) % H}, device_id_type=MESH
        )

    @pl.loop(1, S)
    def _(r):
        pl.semaphore_signal(
            barrier, inc=1, device_id={"seq": (me_s + r) % S}, device_id_type=MESH
        )

    gate_copy = pltpu.make_async_copy(gates_ref, gates, gate_sem)
    gate_copy.start()
    for t, ref in enumerate((q_ref, g_ref, k_ref, v_ref)):
        pltpu.make_async_copy(ref, staged.at[t], in_sem).start()

    t_at = lax.broadcasted_iota(jnp.int32, (T, T), 0)
    s_at = lax.broadcasted_iota(jnp.int32, (T, T), 1)
    causal = t_at >= s_at
    tri = jnp.where(causal, 1.0, 0.0).astype(F32)
    gate_copy.wait()
    c_row = lax.dot_general(
        gates[...], tri, (((1,), (1,)), ((), ())), precision=EXACT, preferred_element_type=F32
    )
    e_col = c_row[:, T - 1 : T]
    norm_col = jnp.sum(jnp.exp(e_col - c_row), axis=1, keepdims=True)
    ends[me_s, 0] = jnp.broadcast_to(norm_col, (NH, DH))
    ends[me_s, 1] = jnp.broadcast_to(e_col, (NH, DH))

    pl.semaphore_wait(barrier, (H - 1) + (S - 1))

    def half(i):
        return pl.ds(pl.multiple_of(2 * i, 2), 2)

    def a2a_copy(h, i, source, target):
        return pltpu.make_async_remote_copy(
            src_ref=staged.at[half(i), :, pl.ds(pl.multiple_of(target * CW + h * DH, DH), DH)],
            dst_ref=rows.at[h, half(i), pl.ds(pl.multiple_of(source * RD, RD), RD), :],
            send_sem=a2a_ssem,
            recv_sem=a2a_rsem.at[h, i],
            device_id={"head": target},
            device_id_type=MESH,
        )

    def own_copy(h, i):
        return pltpu.make_async_copy(
            staged.at[half(i), :, pl.ds(pl.multiple_of(me_h * CW + h * DH, DH), DH)],
            rows.at[h, half(i), pl.ds(pl.multiple_of(me_h * RD, RD), RD), :],
            a2a_rsem.at[h, i],
        )

    def send_half(h, i):
        for r in range(1, H):
            a2a_copy(h, i, me_h, (me_h + r) % H).start()
        own_copy(h, i).start()

    outer = (a == 0) | (a == A - 1)

    def half_step(k):
        n, i = k // 2, k % 2
        late = jnp.where(k < NH, 0, 1)
        ahead = jnp.where(a == 0, 1, 0)
        kind = jnp.where(n == 0, 1 - i, i)
        kind = jnp.where(outer, ahead + late - 2 * ahead * late, kind)
        return jnp.where(outer, k - late * NH, n), kind

    def send_step(k):
        h, kind = half_step(k)
        send_half(h, kind)

    def end_copy(r, source, target):
        return pltpu.make_async_remote_copy(
            src_ref=ends.at[source],
            dst_ref=ends.at[source],
            send_sem=end_ssem,
            recv_sem=end_rsem,
            device_id={"seq": target},
            device_id_type=MESH,
        )

    @pl.loop(1, S)
    def _(r):
        end_copy(r, me_s, (me_s + r) % S).start()

    pltpu.make_async_copy(staged, staged, in_sem).wait()
    send_step(0)

    @pl.loop(1, LEAD)
    def _(k):
        send_step(k)

    if B == 2:
        for i, plane_index in enumerate((A - 1, 0)):
            @pl.when((a == plane_index) & (b == i))
            def _():
                x_recv[:, :, i] = jnp.zeros((B - 1, NH, DH, DH), BF16)

    c_col = c_row.T
    for h in range(NH):
        col = c_col[:, h : h + 1]
        row = c_row[h : h + 1, :]
        decay = jnp.where(causal, jnp.exp(jnp.where(causal, col - row, 0.0)), 0.0)
        table[h] = decay
        grow[h] = jnp.broadcast_to(jnp.exp(col), (T, DH))
        fade[h] = jnp.broadcast_to(jnp.exp(c_col[T - 1 : T, h : h + 1] - col), (T, DH))
        inner[h] = jnp.broadcast_to(jnp.sum(decay, axis=1, keepdims=True), (T, DH))

    def picked(flag, value):
        return jnp.where(flag, 1.0, 0.0) * value

    def take_norm():
        others = ends.at[pl.ds(0, S - 1)]
        pltpu.make_async_copy(others, others, end_rsem).wait()
        gain[3] = lax.fori_loop(
            0,
            me_s,
            lambda m, norm: norm * jnp.exp(ends[m, 1]) + ends[m, 0],
            jnp.zeros((NH, DH), F32),
        )

    def summed(begin, stop, start):
        return lax.fori_loop(begin, stop, lambda m, x: x + ends[m, 1], start)

    def peer(p):
        return lo + (b + p + 1) % B

    def source_peer(p):
        return lo + (b + B - p - 1) % B

    def take_gains():
        zero = jnp.zeros((NH, DH), F32)
        pre = summed(lo, me_s, zero)
        suf = summed(me_s + 1, hi, zero)
        whole = pre + suf + ends[me_s, 1]
        gain[0] = jnp.exp(pre)
        gain[1] = jnp.exp(suf)
        gain[2] = jnp.exp(whole)

        @pl.loop(0, B - 1)
        def _(p):
            other = source_peer(p)
            low = jnp.minimum(me_s, other)
            between = summed(low + 1, jnp.maximum(me_s, other), zero)
            peer_gain[p, 0] = jnp.exp(summed(other + 1, hi, zero))
            peer_gain[p, 1] = picked(other < me_s, jnp.exp(between))
            peer_gain[p, 2] = jnp.exp(summed(lo, other, zero))
            peer_gain[p, 3] = picked(other > me_s, jnp.exp(between))

        @pl.loop(0, A - 1)
        def _(d):
            edge = jnp.where(a == 0, hi, lo - d * B)
            start = jnp.where(a == 0, 1.0, 0.0) * suf + jnp.where(a == 0, 0.0, 1.0) * pre
            stop = jnp.where(a == 0, hi + d * B, lo)

            @pl.when((a == 0) | (a == A - 1))
            def _():
                plane_gain[d] = jnp.exp(summed(edge, stop, start))

    def z_copy(src, dst, ssem, rsem, plane_index):
        return pltpu.make_async_remote_copy(
            src_ref=src,
            dst_ref=dst,
            send_sem=ssem,
            recv_sem=rsem,
            device_id={"seq": plane_index * B + b},
            device_id_type=MESH,
        )

    def y_copy(m):
        return z_copy(y_send.at[m], y_recv.at[m], y_ssem, y_rsem.at[m], (a + 1) % A)

    def n_copy(m):
        return z_copy(n_send.at[m], n_recv.at[m], n_ssem, n_rsem.at[m], (a + A - 1) % A)

    def d_copy(src, ssem, m, slot, target):
        return z_copy(src, d_recv.at[slot, m], ssem, y_rsem.at[m], target)

    def x_copy(p, m, i, target):
        return pltpu.make_async_remote_copy(
            src_ref=x_send.at[m, i],
            dst_ref=x_recv.at[p, m, i],
            send_sem=x_ssem,
            recv_sem=x_rsem.at[m, i],
            device_id={"seq": target},
            device_id_type=MESH,
        )

    idle_plane = A - 1, 0

    def useful(i, taker):
        return (a != idle_plane[i]) | (B > 2) | (taker == 1 - i)

    def x_start(m, i):
        @pl.when(useful(i, 1 - b))
        def _():
            @pl.loop(0, B - 1)
            def _(p):
                x_copy(p, m, i, peer(p)).start()

    def x_wait(m, i):
        @pl.when(useful(i, b))
        def _():
            got = x_recv.at[:, m, i]
            pltpu.make_async_copy(got, got, x_rsem.at[m, i]).wait()

    def weight(index, h):
        return gain[index, pl.ds(h, 1), :]

    def peer_weight(p, index, h):
        return peer_gain[p, index, pl.ds(h, 1), :]

    def arrive(m, i):
        got = rows.at[m, half(i)]
        pltpu.make_async_copy(got, got, a2a_rsem.at[m, i]).wait()

    def key_state(m):
        arrive(m, 1)
        key_fade = (rows[m, 2].astype(F32) * fade[m]).astype(BF16)
        l_state = dot_tn(key_fade, rows[m, 3])
        local[m] = l_state
        x_send[m, 0] = l_state.astype(BF16)
        x_start(m, 0)

    def query_state(m):
        arrive(m, 0)
        growth = grow[m]
        inverse = lax.rsqrt(growth * weight(3, m) + inner[m])
        inner[m] = inverse
        scaled = (rows[m, 1].astype(F32) * inverse).astype(BF16)
        scaled_ref[m] = scaled
        query_growth = (rows[m, 0].astype(F32) * growth).astype(BF16)
        r_state = dot_tn(query_growth, scaled)
        reach[m] = r_state
        x_send[m, 1] = r_state.astype(BF16)
        x_start(m, 1)

    def within(m):
        q, g, k, v = rows[m, 0], rows[m, 1], rows[m, 2], rows[m, 3]
        decay = table[m]
        weighted = (dot_nt(g, v) * decay * inner[m]).astype(BF16)
        affinity = (dot_nt(q, k) * decay).astype(BF16)
        part_q[m] = dot_nn(weighted, k)
        part_k[m] = dot_tn(weighted, q)
        part_v[m] = dot_tn(affinity, scaled_ref[m])

    def plane_n(m):
        x_wait(m, 1)
        total = fold(
            B - 1,
            lambda p, x: x + peer_weight(p, 2, m) * x_recv[p, m, 1].astype(F32),
            weight(0, m) * reach[m],
        )

        @pl.when(a == 2)
        def _():
            sum_n[m] = total

        @pl.when(a != 2)
        def _():
            n_send[m] = total.astype(BF16)

        @pl.when(a == 1)
        def _():
            d_copy(n_send.at[m], n_ssem, m, 0, 0).start()

        @pl.when(a == 3)
        def _():
            n_copy(m).start()

    def plane_p(m):
        x_wait(m, 0)
        total = fold(
            B - 1,
            lambda p, x: x + peer_weight(p, 0, m) * x_recv[p, m, 0].astype(F32),
            weight(1, m) * local[m],
        )

        @pl.when(a == 1)
        def _():
            sum_p[m] = total

        @pl.when(a != 1)
        def _():
            y_send[m] = total.astype(BF16)

        @pl.when(a == 0)
        def _():
            y_copy(m).start()

        @pl.when(a == 2)
        def _():
            d_copy(y_send.at[m], y_ssem, m, 0, A - 1).start()

    def hop_up(m):
        y_copy(m).wait_recv()
        y_send[m] = (sum_p[m] + weight(2, m) * y_recv[m].astype(F32)).astype(BF16)
        d_copy(y_send.at[m], y_ssem, m, 1, A - 1).start()
        y_copy(m).start()

    def hop_down(m):
        n_copy(m).wait_recv()
        n_send[m] = (sum_n[m] + weight(2, m) * n_recv[m].astype(F32)).astype(BF16)
        d_copy(n_send.at[m], n_ssem, m, 1, 0).start()
        n_copy(m).start()

    def hop(m):
        @pl.when(a == 1)
        def _():
            hop_up(m)

        @pl.when(a == 2)
        def _():
            hop_down(m)

    def direct(m, count):
        got = d_recv.at[pl.ds(0, count), m]
        pltpu.make_async_copy(got, got, y_rsem.at[m]).wait()
        total = plane_gain[0, pl.ds(m, 1), :] * d_recv[0, m].astype(F32)
        for d in range(1, count):
            total += plane_gain[d, pl.ds(m, 1), :] * d_recv[d, m].astype(F32)
        return total

    def finish(m):
        @pl.when(a == 2)
        def _():
            y_copy(m).wait_recv()

        @pl.when(a == 1)
        def _():
            n_copy(m).wait_recv()

        @pl.when((a == 1) | (a == 2))
        def _():
            acc_p[...] = weight(0, m) * y_recv[m].astype(F32)
            acc_n[...] = weight(1, m) * n_recv[m].astype(F32)

        @pl.when(a == A - 1)
        def _():
            x_wait(m, 0)
            acc_p[...] = direct(m, 2)
            acc_n[...] = jnp.zeros_like(acc_n)

        @pl.when(a == 0)
        def _():
            x_wait(m, 1)
            acc_p[...] = jnp.zeros_like(acc_p)
            acc_n[...] = direct(m, 2)

        prefix = fold(
            B - 1,
            lambda p, x: x + peer_weight(p, 1, m) * x_recv[p, m, 0].astype(F32),
            acc_p[...],
        ).astype(BF16)
        later = fold(
            B - 1,
            lambda p, x: x + peer_weight(p, 3, m) * x_recv[p, m, 1].astype(F32),
            acc_n[...],
        ).astype(BF16)
        gq = part_q[m] + grow[m] * dot_nt(scaled_ref[m], prefix)
        gk = part_k[m] + fade[m] * dot_nt(rows[m, 3], later)
        gv = part_v[m] + fade[m] * dot_nn(rows[m, 2], later)
        at = pl.ds(pl.multiple_of(m * DH, DH), DH)
        gq_ref[:, at] = gq.astype(BF16)
        gk_ref[:, at] = gk.astype(BF16)
        gv_ref[:, at] = gv.astype(BF16)

    def guarded(do, m, limit):
        @pl.when((m >= 0) & (m < limit))
        def _():
            do(m)

    def by_plane(values):
        return sum(jnp.where(a == i, value, 0) for i, value in enumerate(values))

    fin_lag = by_plane(FINS)
    p_count, n_count = by_plane((2, 1, 1, 0)), by_plane((0, 1, 1, 2))
    pair = jnp.where(outer, 2, 1)

    def several(do, begin, count):
        @pl.when((begin >= 0) & (begin < NH))
        def _():
            @pl.loop(0, count)
            def _(i):
                do(begin + i)

    def state_step(k):
        h, kind = half_step(k)

        @pl.when(kind == 1)
        def _():
            key_state(h)

        @pl.when(kind == 0)
        def _():
            query_state(h)

    @pl.loop(0, NH + fin_lag)
    def _(n):
        @pl.when(n < NH)
        def _():
            @pl.loop(0, 2)
            def _(i):
                k = 2 * n + i

                @pl.when(k == jnp.where(a == A - 1, 0, 1))
                def _():
                    take_norm()

                @pl.when(k + LEAD < 2 * NH)
                def _():
                    send_step(k + LEAD)

                state_step(k)

            @pl.when(n == 0)
            def _():
                take_gains()

        group = jnp.where(outer, 2 * (n - XLAG), n - XLAG)
        several(plane_n, group, n_count)
        several(plane_p, group, p_count)
        several(hop, n - by_plane(HOPS), jnp.where(outer, 0, 1))
        several(within, jnp.where(outer, 2 * n - NH, n), pair)
        guarded(finish, n - fin_lag, NH)

    others = ends.at[pl.ds(0, S - 1)]
    pltpu.make_async_copy(others, others, end_ssem).wait()
    sent = staged.at[:, :, pl.ds(0, (H - 1) * CW)]
    pltpu.make_async_copy(sent, sent, a2a_ssem).wait()
    sent_both = useful(0, 1 - b) & useful(1, 1 - b)

    @pl.when(sent_both)
    def _():
        pltpu.make_async_copy(x_recv, x_recv, x_ssem).wait()

    @pl.when(jnp.logical_not(sent_both))
    def _():
        one_kind = x_recv.at[:, :, 0]
        pltpu.make_async_copy(one_kind, one_kind, x_ssem).wait()


    def sent_all(ref, sem):
        pltpu.make_async_copy(ref, ref, sem).wait()

    @pl.when((a == 0) | (a == 2))
    def _():
        sent_all(d_recv.at[0], y_ssem)

    @pl.when(a == 1)
    def _():
        sent_all(d_recv.at[pl.ds(0, 2)], y_ssem)

    @pl.when((a == 1) | (a == 3))
    def _():
        sent_all(d_recv.at[0], n_ssem)

    @pl.when(a == 2)
    def _():
        sent_all(d_recv.at[pl.ds(0, 2)], n_ssem)


def hand_over(x_ref, y_ref, z_ref, x_out, y_out, z_out, sems):
    sources, targets = (x_ref, y_ref, z_ref), (x_out, y_out, z_out)
    stores = [pltpu.make_async_copy(sources[i], targets[i], sems.at[i]) for i in range(3)]
    for store in stores:
        store.start()
    for store in stores:
        store.wait()


def body(seq_size, head_size, queries, keys, values, grad_out, gates):
    S, H = seq_size, head_size
    B = S // SLOW
    RD, width = queries.shape
    T = RD * H
    CW = width // H
    NH = CW // DH
    square = (NH, T, DH)
    state = (NH, DH, DH)
    one = (DH, DH)
    vmem = pltpu.VMEM
    dma = pltpu.SemaphoreType.DMA
    anywhere = pl.BlockSpec(memory_space=pl.ANY)
    in_hbm = pl.BlockSpec(memory_space=pltpu.HBM)
    out = jax.ShapeDtypeStruct((T, CW), BF16)
    kept = pltpu.VMEM((T, CW), BF16)
    inputs = [
        pltpu.with_memory_space_constraint(x, pltpu.HBM)
        for x in (queries, keys, values, grad_out, gates.T)
    ]
    results = pl.pallas_call(
        functools.partial(kernel, S, H),
        out_shape=(kept, kept, kept),
        in_specs=[in_hbm] * 5,
        out_specs=(pl.BlockSpec(memory_space=pltpu.VMEM),) * 3,
        scratch_shapes=[
            vmem((NH, T), F32),
            vmem((4, RD, width), BF16),
            vmem((NH, 4, T, DH), BF16),
            vmem((S, 2, NH, DH), F32),
            vmem((4, NH, DH), F32),
            vmem((B - 1, 4, NH, DH), F32),
            vmem((SLOW - 1, NH, DH), F32),
            vmem((NH, T, T), F32),
            vmem(square, F32),
            vmem(square, F32),
            vmem(square, F32),
            vmem(square, BF16),
            vmem(state, F32),
            vmem(state, F32),
            vmem(state, F32),
            vmem(state, F32),
            vmem(square, F32),
            vmem(square, F32),
            vmem(square, F32),
            vmem((NH, 2) + one, BF16),
            vmem((B - 1, NH, 2) + one, BF16),
            vmem(state, BF16),
            vmem(state, BF16),
            vmem(state, BF16),
            vmem(state, BF16),
            vmem((SLOW - 1,) + state, BF16),
            vmem(one, F32),
            vmem(one, F32),
            dma,
            dma,
            dma,
            dma((NH, 2)),
            dma,
            dma,
            dma,
            dma((NH, 2)),
            dma,
            dma((NH,)),
            dma,
            dma((NH,)),
        ],
        compiler_params=pltpu.CompilerParams(
            collective_id=0,
            has_side_effects=True,
            vmem_limit_bytes=24 << 20,
        ),
    )(*inputs)
    return pl.pallas_call(
        hand_over,
        out_shape=(out, out, out),
        in_specs=[anywhere] * 3,
        out_specs=(in_hbm,) * 3,
        scratch_shapes=[dma((3,))],
        compiler_params=pltpu.CompilerParams(vmem_limit_bytes=4 << 20),
    )(*results)


def solution(mesh):
    placed = (
        P(("seq", "head"), None),
        P(("seq", "head"), None),
        P(("seq", "head"), None),
        P(("seq", "head"), None),
        P("seq", "head"),
    )
    return jax.shard_map(
        functools.partial(body, mesh.shape["seq"], mesh.shape["head"]),
        mesh=mesh,
        in_specs=placed,
        out_specs=(P("seq", "head"), P("seq", "head"), P("seq", "head")),
        check_vma=False,
    )
```

```python
import functools

import jax
import jax.numpy as jnp
from jax import lax
from jax.experimental import pallas as pl
from jax.experimental.pallas import tpu as pltpu
from jax.sharding import PartitionSpec as P

DH = 128
SLOW = 4
XLAG = 3
HOPS = (0, 4, 4, 0)
FINS = (10, 11, 11, 10)
LEAD = 8
PARTS = 4

MESH = pl.DeviceIdType.MESH
F32 = jnp.float32
BF16 = jnp.bfloat16
EXACT = lax.Precision.HIGHEST


def dot_nn(x, y):
    return lax.dot_general(x, y, (((1,), (0,)), ((), ())), preferred_element_type=F32)


def dot_nt(x, y):
    return lax.dot_general(x, y, (((1,), (1,)), ((), ())), preferred_element_type=F32)


def dot_tn(x, y):
    return lax.dot_general(x, y, (((0,), (0,)), ((), ())), preferred_element_type=F32)


def fold(count, step, start):
    return step(0, start) if count == 1 else lax.fori_loop(0, count, step, start)


def kernel(
    seq_size, head_size,
    q_ref, k_ref, v_ref, g_ref, gates_ref,
    gq_ref, gk_ref, gv_ref,
    gates, staged, rows, ends, gain, peer_gain, plane_gain,
    table, grow, fade, inner, scaled_ref,
    local, reach, sum_p, sum_n, part_q, part_k, part_v,
    x_send, x_recv, y_send, y_recv, n_send, n_recv, d_recv, acc_p, acc_n,
    in_sem, gate_sem, a2a_ssem, a2a_rsem, end_ssem, end_rsem,
    x_ssem, x_rsem, y_ssem, y_rsem, n_ssem, n_rsem,
):
    S, H = seq_size, head_size
    A = SLOW
    B = S // A
    RD = q_ref.shape[0]
    T = RD * H
    CW = q_ref.shape[1] // H
    NH = CW // DH
    me_s = lax.axis_index("seq")
    me_h = lax.axis_index("head")
    a = me_s // B
    b = me_s % B
    lo = a * B
    hi = lo + B

    barrier = pltpu.get_barrier_semaphore()
    for r in range(1, H):
        pl.semaphore_signal(
            barrier, inc=1, device_id={"head": (me_h + r) % H}, device_id_type=MESH
        )

    @pl.loop(1, S)
    def _(r):
        pl.semaphore_signal(
            barrier, inc=1, device_id={"seq": (me_s + r) % S}, device_id_type=MESH
        )

    gate_copy = pltpu.make_async_copy(gates_ref, gates, gate_sem)
    gate_copy.start()
    for t, ref in enumerate((q_ref, g_ref, k_ref, v_ref)):
        pltpu.make_async_copy(ref, staged.at[t], in_sem).start()

    t_at = lax.broadcasted_iota(jnp.int32, (T, T), 0)
    s_at = lax.broadcasted_iota(jnp.int32, (T, T), 1)
    causal = t_at >= s_at
    tri = jnp.where(causal, 1.0, 0.0).astype(F32)
    gate_copy.wait()
    c_row = lax.dot_general(
        gates[...], tri, (((1,), (1,)), ((), ())), precision=EXACT, preferred_element_type=F32
    )
    e_col = c_row[:, T - 1 : T]
    norm_col = jnp.sum(jnp.exp(e_col - c_row), axis=1, keepdims=True)
    ends[me_s, 0] = jnp.broadcast_to(norm_col, (NH, DH))
    ends[me_s, 1] = jnp.broadcast_to(e_col, (NH, DH))

    pl.semaphore_wait(barrier, (H - 1) + (S - 1))

    def half(i):
        return pl.ds(pl.multiple_of(2 * i, 2), 2)

    def a2a_copy(h, i, source, target):
        return pltpu.make_async_remote_copy(
            src_ref=staged.at[half(i), :, pl.ds(pl.multiple_of(target * CW + h * DH, DH), DH)],
            dst_ref=rows.at[h, half(i), pl.ds(pl.multiple_of(source * RD, RD), RD), :],
            send_sem=a2a_ssem,
            recv_sem=a2a_rsem.at[h, i],
            device_id={"head": target},
            device_id_type=MESH,
        )

    def own_copy(h, i):
        return pltpu.make_async_copy(
            staged.at[half(i), :, pl.ds(pl.multiple_of(me_h * CW + h * DH, DH), DH)],
            rows.at[h, half(i), pl.ds(pl.multiple_of(me_h * RD, RD), RD), :],
            a2a_rsem.at[h, i],
        )

    def send_half(h, i):
        for r in range(1, H):
            a2a_copy(h, i, me_h, (me_h + r) % H).start()
        own_copy(h, i).start()

    outer = (a == 0) | (a == A - 1)

    def half_step(k):
        n, i = k // 2, k % 2
        late = jnp.where(k < NH, 0, 1)
        ahead = jnp.where(a == 0, 1, 0)
        kind = jnp.where((n == 0) | (a == 1), 1 - i, i)
        kind = jnp.where(outer, ahead + late - 2 * ahead * late, kind)
        return jnp.where(outer, k - late * NH, n), kind

    def send_step(k):
        h, kind = half_step(k)
        send_half(h, kind)

    def end_copy(r, source, target):
        return pltpu.make_async_remote_copy(
            src_ref=ends.at[source],
            dst_ref=ends.at[source],
            send_sem=end_ssem,
            recv_sem=end_rsem,
            device_id={"seq": target},
            device_id_type=MESH,
        )

    @pl.loop(1, S)
    def _(r):
        end_copy(r, me_s, (me_s + r) % S).start()

    pltpu.make_async_copy(staged, staged, in_sem).wait()
    send_step(0)

    @pl.loop(1, LEAD)
    def _(k):
        send_step(k)

    if B == 2:
        for i, plane_index in enumerate((A - 1, 0)):
            @pl.when((a == plane_index) & (b == i))
            def _():
                x_recv[:, :, i] = jnp.zeros((B - 1, NH, DH, DH), BF16)

    c_col = c_row.T
    for h in range(NH):
        col = c_col[:, h : h + 1]
        row = c_row[h : h + 1, :]
        decay = jnp.where(causal, jnp.exp(jnp.where(causal, col - row, 0.0)), 0.0)
        table[h] = decay
        grow[h] = jnp.broadcast_to(jnp.exp(col), (T, DH))
        fade[h] = jnp.broadcast_to(jnp.exp(c_col[T - 1 : T, h : h + 1] - col), (T, DH))
        inner[h] = jnp.broadcast_to(jnp.sum(decay, axis=1, keepdims=True), (T, DH))

    def picked(flag, value):
        return jnp.where(flag, 1.0, 0.0) * value

    def take_norm():
        others = ends.at[pl.ds(0, S - 1)]
        pltpu.make_async_copy(others, others, end_rsem).wait()
        gain[3] = lax.fori_loop(
            0,
            me_s,
            lambda m, norm: norm * jnp.exp(ends[m, 1]) + ends[m, 0],
            jnp.zeros((NH, DH), F32),
        )

    def summed(begin, stop, start):
        return lax.fori_loop(begin, stop, lambda m, x: x + ends[m, 1], start)

    def peer(p):
        return lo + (b + p + 1) % B

    def source_peer(p):
        return lo + (b + B - p - 1) % B

    def take_gains():
        zero = jnp.zeros((NH, DH), F32)
        pre = summed(lo, me_s, zero)
        suf = summed(me_s + 1, hi, zero)
        whole = pre + suf + ends[me_s, 1]
        gain[0] = jnp.exp(pre)
        gain[1] = jnp.exp(suf)
        gain[2] = jnp.exp(whole)

        @pl.loop(0, B - 1)
        def _(p):
            other = source_peer(p)
            low = jnp.minimum(me_s, other)
            between = summed(low + 1, jnp.maximum(me_s, other), zero)
            peer_gain[p, 0] = jnp.exp(summed(other + 1, hi, zero))
            peer_gain[p, 1] = picked(other < me_s, jnp.exp(between))
            peer_gain[p, 2] = jnp.exp(summed(lo, other, zero))
            peer_gain[p, 3] = picked(other > me_s, jnp.exp(between))

        @pl.loop(0, A - 1)
        def _(d):
            edge = jnp.where(a == 0, hi, lo - d * B)
            start = jnp.where(a == 0, 1.0, 0.0) * suf + jnp.where(a == 0, 0.0, 1.0) * pre
            stop = jnp.where(a == 0, hi + d * B, lo)

            @pl.when((a == 0) | (a == A - 1))
            def _():
                plane_gain[d] = jnp.exp(summed(edge, stop, start))

    def z_copy(src, dst, ssem, rsem, plane_index):
        return pltpu.make_async_remote_copy(
            src_ref=src,
            dst_ref=dst,
            send_sem=ssem,
            recv_sem=rsem,
            device_id={"seq": plane_index * B + b},
            device_id_type=MESH,
        )

    def y_copy(m):
        return z_copy(y_send.at[m], y_recv.at[m], y_ssem, y_rsem.at[m], (a + 1) % A)

    def n_copy(m):
        return z_copy(n_send.at[m], n_recv.at[m], n_ssem, n_rsem.at[m], (a + A - 1) % A)

    def d_copy(src, ssem, m, slot, target):
        return z_copy(src, d_recv.at[slot, m], ssem, y_rsem.at[m], target)

    def x_copy(p, m, i, target):
        return pltpu.make_async_remote_copy(
            src_ref=x_send.at[m, i],
            dst_ref=x_recv.at[p, m, i],
            send_sem=x_ssem,
            recv_sem=x_rsem.at[m, i],
            device_id={"seq": target},
            device_id_type=MESH,
        )

    idle_plane = A - 1, 0

    def useful(i, taker):
        return (a != idle_plane[i]) | (B > 2) | (taker == 1 - i)

    def x_start(m, i):
        @pl.when(useful(i, 1 - b))
        def _():
            @pl.loop(0, B - 1)
            def _(p):
                x_copy(p, m, i, peer(p)).start()

    def x_wait(m, i):
        @pl.when(useful(i, b))
        def _():
            got = x_recv.at[:, m, i]
            pltpu.make_async_copy(got, got, x_rsem.at[m, i]).wait()

    def weight(index, h):
        return gain[index, pl.ds(h, 1), :]

    def peer_weight(p, index, h):
        return peer_gain[p, index, pl.ds(h, 1), :]

    def arrive(m, i):
        got = rows.at[m, half(i)]
        pltpu.make_async_copy(got, got, a2a_rsem.at[m, i]).wait()

    def key_state(m):
        arrive(m, 1)
        key_fade = (rows[m, 2].astype(F32) * fade[m]).astype(BF16)
        l_state = dot_tn(key_fade, rows[m, 3])
        local[m] = l_state
        x_send[m, 0] = l_state.astype(BF16)
        x_start(m, 0)

    def query_state(m):
        arrive(m, 0)
        growth = grow[m]
        inverse = lax.rsqrt(growth * weight(3, m) + inner[m])
        inner[m] = inverse
        scaled = (rows[m, 1].astype(F32) * inverse).astype(BF16)
        scaled_ref[m] = scaled
        query_growth = (rows[m, 0].astype(F32) * growth).astype(BF16)
        r_state = dot_tn(query_growth, scaled)
        reach[m] = r_state
        x_send[m, 1] = r_state.astype(BF16)
        x_start(m, 1)

    def within(m):
        q, g, k, v = rows[m, 0], rows[m, 1], rows[m, 2], rows[m, 3]
        decay = table[m]
        weighted = (dot_nt(g, v) * decay * inner[m]).astype(BF16)
        affinity = (dot_nt(q, k) * decay).astype(BF16)
        part_q[m] = dot_nn(weighted, k)
        part_k[m] = dot_tn(weighted, q)
        part_v[m] = dot_tn(affinity, scaled_ref[m])

    def plane_n(m):
        x_wait(m, 1)
        total = fold(
            B - 1,
            lambda p, x: x + peer_weight(p, 2, m) * x_recv[p, m, 1].astype(F32),
            weight(0, m) * reach[m],
        )

        @pl.when(a == 2)
        def _():
            sum_n[m] = total

        @pl.when(a != 2)
        def _():
            n_send[m] = total.astype(BF16)

        @pl.when(a == 1)
        def _():
            d_copy(n_send.at[m], n_ssem, m, 0, 0).start()

        @pl.when(a == 3)
        def _():
            n_copy(m).start()

    def plane_p(m):
        x_wait(m, 0)
        total = fold(
            B - 1,
            lambda p, x: x + peer_weight(p, 0, m) * x_recv[p, m, 0].astype(F32),
            weight(1, m) * local[m],
        )

        @pl.when(a == 1)
        def _():
            sum_p[m] = total

        @pl.when(a != 1)
        def _():
            y_send[m] = total.astype(BF16)

        @pl.when(a == 0)
        def _():
            y_copy(m).start()

        @pl.when(a == 2)
        def _():
            d_copy(y_send.at[m], y_ssem, m, 0, A - 1).start()

    def hop_up(m):
        y_copy(m).wait_recv()
        y_send[m] = (sum_p[m] + weight(2, m) * y_recv[m].astype(F32)).astype(BF16)
        d_copy(y_send.at[m], y_ssem, m, 1, A - 1).start()
        y_copy(m).start()

    def hop_down(m):
        n_copy(m).wait_recv()
        n_send[m] = (sum_n[m] + weight(2, m) * n_recv[m].astype(F32)).astype(BF16)
        d_copy(n_send.at[m], n_ssem, m, 1, 0).start()
        n_copy(m).start()

    def hop(m):
        @pl.when(a == 1)
        def _():
            hop_up(m)

        @pl.when(a == 2)
        def _():
            hop_down(m)

    def direct(m, count):
        got = d_recv.at[pl.ds(0, count), m]
        pltpu.make_async_copy(got, got, y_rsem.at[m]).wait()
        total = plane_gain[0, pl.ds(m, 1), :] * d_recv[0, m].astype(F32)
        for d in range(1, count):
            total += plane_gain[d, pl.ds(m, 1), :] * d_recv[d, m].astype(F32)
        return total

    def finish(m):
        @pl.when(a == 2)
        def _():
            y_copy(m).wait_recv()

        @pl.when(a == 1)
        def _():
            n_copy(m).wait_recv()

        @pl.when((a == 1) | (a == 2))
        def _():
            acc_p[...] = weight(0, m) * y_recv[m].astype(F32)
            acc_n[...] = weight(1, m) * n_recv[m].astype(F32)

        @pl.when(a == A - 1)
        def _():
            x_wait(m, 0)
            acc_p[...] = direct(m, 2)
            acc_n[...] = jnp.zeros_like(acc_n)

        @pl.when(a == 0)
        def _():
            x_wait(m, 1)
            acc_p[...] = jnp.zeros_like(acc_p)
            acc_n[...] = direct(m, 2)

        prefix = fold(
            B - 1,
            lambda p, x: x + peer_weight(p, 1, m) * x_recv[p, m, 0].astype(F32),
            acc_p[...],
        ).astype(BF16)
        later = fold(
            B - 1,
            lambda p, x: x + peer_weight(p, 3, m) * x_recv[p, m, 1].astype(F32),
            acc_n[...],
        ).astype(BF16)
        gq = part_q[m] + grow[m] * dot_nt(scaled_ref[m], prefix)
        gk = part_k[m] + fade[m] * dot_nt(rows[m, 3], later)
        gv = part_v[m] + fade[m] * dot_nn(rows[m, 2], later)
        at = pl.ds(pl.multiple_of(m * DH, DH), DH)
        gq_ref[:, at] = gq.astype(BF16)
        gk_ref[:, at] = gk.astype(BF16)
        gv_ref[:, at] = gv.astype(BF16)

    def guarded(do, m, limit):
        @pl.when((m >= 0) & (m < limit))
        def _():
            do(m)

    def by_plane(values):
        return sum(jnp.where(a == i, value, 0) for i, value in enumerate(values))

    fin_lag = by_plane(FINS)
    p_count, n_count = by_plane((2, 1, 1, 0)), by_plane((0, 1, 1, 2))
    pair = jnp.where(outer, 2, 1)

    def several(do, begin, count):
        @pl.when((begin >= 0) & (begin < NH))
        def _():
            @pl.loop(0, count)
            def _(i):
                do(begin + i)

    def state_step(k):
        h, kind = half_step(k)

        @pl.when(kind == 1)
        def _():
            key_state(h)

        @pl.when(kind == 0)
        def _():
            query_state(h)

    @pl.loop(0, NH + fin_lag)
    def _(n):
        @pl.when(n < NH)
        def _():
            @pl.loop(0, 2)
            def _(i):
                k = 2 * n + i

                @pl.when(k == jnp.where(a == A - 1, 0, 1))
                def _():
                    take_norm()

                @pl.when(k + LEAD < 2 * NH)
                def _():
                    send_step(k + LEAD)

                state_step(k)

            @pl.when(n == 0)
            def _():
                take_gains()

        group = jnp.where(outer, 2 * (n - XLAG), n - XLAG)
        several(plane_n, group, n_count)
        several(plane_p, group, p_count)
        several(hop, n - by_plane(HOPS), jnp.where(outer, 0, 1))
        several(within, jnp.where(outer, 2 * n - NH, n), pair)
        guarded(finish, n - fin_lag, NH)

    others = ends.at[pl.ds(0, S - 1)]
    pltpu.make_async_copy(others, others, end_ssem).wait()
    sent = staged.at[:, :, pl.ds(0, (H - 1) * CW)]
    pltpu.make_async_copy(sent, sent, a2a_ssem).wait()
    sent_both = useful(0, 1 - b) & useful(1, 1 - b)

    @pl.when(sent_both)
    def _():
        pltpu.make_async_copy(x_recv, x_recv, x_ssem).wait()

    @pl.when(jnp.logical_not(sent_both))
    def _():
        one_kind = x_recv.at[:, :, 0]
        pltpu.make_async_copy(one_kind, one_kind, x_ssem).wait()


    def sent_all(ref, sem):
        pltpu.make_async_copy(ref, ref, sem).wait()

    @pl.when((a == 0) | (a == 2))
    def _():
        sent_all(d_recv.at[0], y_ssem)

    @pl.when(a == 1)
    def _():
        sent_all(d_recv.at[pl.ds(0, 2)], y_ssem)

    @pl.when((a == 1) | (a == 3))
    def _():
        sent_all(d_recv.at[0], n_ssem)

    @pl.when(a == 2)
    def _():
        sent_all(d_recv.at[pl.ds(0, 2)], n_ssem)


def hand_over(x_ref, y_ref, z_ref, x_out, y_out, z_out, sems):
    pairs = ((x_ref, x_out), (y_ref, y_out), (z_ref, z_out))
    size = x_ref.shape[0] // PARTS
    for part in range(PARTS):
        at = pl.ds(part * size, size)
        for i, (source, target) in enumerate(pairs):
            pltpu.make_async_copy(source.at[at], target.at[at], sems.at[i]).start()
    for i, (source, target) in enumerate(pairs):
        pltpu.make_async_copy(source, target, sems.at[i]).wait()


def body(seq_size, head_size, queries, keys, values, grad_out, gates):
    S, H = seq_size, head_size
    B = S // SLOW
    RD, width = queries.shape
    T = RD * H
    CW = width // H
    NH = CW // DH
    square = (NH, T, DH)
    state = (NH, DH, DH)
    one = (DH, DH)
    vmem = pltpu.VMEM
    dma = pltpu.SemaphoreType.DMA
    anywhere = pl.BlockSpec(memory_space=pl.ANY)
    in_hbm = pl.BlockSpec(memory_space=pltpu.HBM)
    out = jax.ShapeDtypeStruct((T, CW), BF16)
    kept = pltpu.VMEM((T, CW), BF16)
    inputs = [
        pltpu.with_memory_space_constraint(x, pltpu.HBM)
        for x in (queries, keys, values, grad_out, gates.T)
    ]
    results = pl.pallas_call(
        functools.partial(kernel, S, H),
        out_shape=(kept, kept, kept),
        in_specs=[in_hbm] * 5,
        out_specs=(pl.BlockSpec(memory_space=pltpu.VMEM),) * 3,
        scratch_shapes=[
            vmem((NH, T), F32),
            vmem((4, RD, width), BF16),
            vmem((NH, 4, T, DH), BF16),
            vmem((S, 2, NH, DH), F32),
            vmem((4, NH, DH), F32),
            vmem((B - 1, 4, NH, DH), F32),
            vmem((SLOW - 1, NH, DH), F32),
            vmem((NH, T, T), F32),
            vmem(square, F32),
            vmem(square, F32),
            vmem(square, F32),
            vmem(square, BF16),
            vmem(state, F32),
            vmem(state, F32),
            vmem(state, F32),
            vmem(state, F32),
            vmem(square, F32),
            vmem(square, F32),
            vmem(square, F32),
            vmem((NH, 2) + one, BF16),
            vmem((B - 1, NH, 2) + one, BF16),
            vmem(state, BF16),
            vmem(state, BF16),
            vmem(state, BF16),
            vmem(state, BF16),
            vmem((SLOW - 1,) + state, BF16),
            vmem(one, F32),
            vmem(one, F32),
            dma,
            dma,
            dma,
            dma((NH, 2)),
            dma,
            dma,
            dma,
            dma((NH, 2)),
            dma,
            dma((NH,)),
            dma,
            dma((NH,)),
        ],
        compiler_params=pltpu.CompilerParams(
            collective_id=0,
            has_side_effects=True,
            vmem_limit_bytes=24 << 20,
        ),
    )(*inputs)
    return pl.pallas_call(
        hand_over,
        out_shape=(out, out, out),
        in_specs=[anywhere] * 3,
        out_specs=(in_hbm,) * 3,
        scratch_shapes=[dma((3,))],
        compiler_params=pltpu.CompilerParams(vmem_limit_bytes=4 << 20),
    )(*results)


def solution(mesh):
    placed = (
        P(("seq", "head"), None),
        P(("seq", "head"), None),
        P(("seq", "head"), None),
        P(("seq", "head"), None),
        P("seq", "head"),
    )
    return jax.shard_map(
        functools.partial(body, mesh.shape["seq"], mesh.shape["head"]),
        mesh=mesh,
        in_specs=placed,
        out_specs=(P("seq", "head"), P("seq", "head"), P("seq", "head")),
        check_vma=False,
    )
```
